512 devices in a mesh: row: 32 (over x, y_lo, core), col: 16 (over y_hi, z).
Axes of the slice: x: 4, y: 8 (y_hi: 2, y_lo: 4; y = y_hi * 4 + y_lo), z: 8, core: 2. Of those that a mesh axis runs over, the one named last changes fastest.
Arguments:
- tile_entries: float32 [32, 16, 64, 128, 128], P('row', 'col'), may hold values from 0 to 65520, as said below
- tile_rows: int32 [32, 16, 64], P('row', 'col'), may hold values from 0 to 31, as said below
- tile_cols: int32 [32, 16, 64], P('row', 'col'), may hold values from 0 to 63, as said below
- tile_count: int32 [32, 16], P('row', 'col'), may hold values from 8 to 64, as said below
- block_x: float32 [64, 131072], P(None, ('row', 'col')), may hold values from 0 to 65520, as said below
- block_y: float32 [64, 131072], P(None, ('row', 'col')), may hold values from 0 to 65520, as said below
Outputs:
- matrix_poly: float32 [3, 64, 64], replicated
- vector_last: float32 [64, 131072], P(None, ('row', 'col'))
The draws below stay inside these ranges and needn't reach their ends.
Inputs may be any that keep to these rules, and one draw needn't show every extreme that they name: `tile_entries`: whole numbers. `block_x`: whole numbers. `block_y`: whole numbers. The slots of one device name distinct block pairs (tile_rows, tile_cols), among them (0, 0) and (31, 63) in some slot. `tile_cols`: block column k of column group c is the global block column (k // 2) * 32 + c * 2 + k % 2. Slots 0 to tile_count - 1 of a device hold its tiles, the rest are unused; some device fills all 64 slots.
All inputs are finite; a program needn't handle non-finite values.
Results may differ from the reference program's by a relative error of at most 0.0003.
Values sent between devices are 32-bit elements; how exact they have to be, the bound alone decides.
A program may use at most 64 MiB of HBM per device.

```python
import jax
import jax.numpy as jnp
from jax import lax

TILE_SIZE = 128
BLOCK_WIDTH = 64
PIECE_BLOCKS = 2
SLOTS = 64
STEP_COUNT = 3
ROW_BLOCKS = 32
COL_BLOCKS = 64
ALL_BLOCKS = 1024
MATRIX_ORDER = 131072
N_ROW = 32
N_COL = 16


def slot_positions(key):
    base_key = jax.random.fold_in(key, 7)
    cell_count = ROW_BLOCKS * COL_BLOCKS
    device_total = N_ROW * N_COL

    def one_device(device_key):
        perm_key, shuffle_key = jax.random.split(device_key)
        middle = jax.random.permutation(perm_key, cell_count - 2)[:SLOTS - 2] + 1
        listed = jnp.concatenate([jnp.array([0, cell_count - 1], jnp.int32), middle.astype(jnp.int32)])
        shuffle = jax.random.permutation(shuffle_key, SLOTS)
        return listed[shuffle]
    device_keys = jax.random.split(base_key, device_total)
    return jax.vmap(one_device)(device_keys).reshape(N_ROW, N_COL, SLOTS)


def draw_tile_rows(key, part):
    return (slot_positions(key) // COL_BLOCKS).astype(jnp.int32)


def draw_tile_cols(key, part):
    return (slot_positions(key) % COL_BLOCKS).astype(jnp.int32)


def draw_tile_count(key, part):
    base_key = jax.random.fold_in(key, 11)
    key_first, key_second, key_busy, key_other = jax.random.split(base_key, 4)
    device_total = N_ROW * N_COL
    least_count = max(SLOTS // 8, 1)
    first_draw = jax.random.randint(key_first, (device_total,), 0, SLOTS)
    second_draw = jax.random.randint(key_second, (device_total,), 0, SLOTS)
    counts = jnp.clip(jnp.minimum(first_draw, second_draw) + 1, least_count, SLOTS)
    busiest = jax.random.randint(key_busy, (), 0, device_total)
    other_device = (busiest + 1 + jax.random.randint(key_other, (), 0, device_total - 1)) % device_total
    device_ids = jnp.arange(device_total)
    counts = jnp.where(device_ids == busiest, SLOTS, jnp.where(device_ids == other_device, least_count, counts))
    return counts.reshape(N_ROW, N_COL).astype(jnp.int32)


def draw_tile_entries(key, part):
    values = jax.random.randint(jax.random.fold_in(key, 3), (N_ROW, N_COL, SLOTS, TILE_SIZE, TILE_SIZE), 0, 65521)
    return values.astype(jnp.float32)


def draw_block_x(key, part):
    values = jax.random.randint(jax.random.fold_in(key, 5), (BLOCK_WIDTH, MATRIX_ORDER), 0, 65521)
    return values.astype(jnp.float32)


def draw_block_y(key, part):
    values = jax.random.randint(jax.random.fold_in(key, 9), (BLOCK_WIDTH, MATRIX_ORDER), 0, 65521)
    return values.astype(jnp.float32)


def setup_inputs(seed: int = 0) -> dict:
    arg_keys = jax.random.split(jax.random.key(seed), 7)
    return {
        "tile_entries": draw_tile_entries(jax.random.fold_in(arg_keys[6], 71), 0),
        "tile_rows": draw_tile_rows(jax.random.fold_in(arg_keys[6], 71), 0),
        "tile_cols": draw_tile_cols(jax.random.fold_in(arg_keys[6], 71), 0),
        "tile_count": draw_tile_count(jax.random.fold_in(arg_keys[6], 71), 0),
        "block_x": draw_block_x(jax.random.fold_in(arg_keys[6], 71), 0),
        "block_y": draw_block_y(jax.random.fold_in(arg_keys[6], 71), 0),
    }


MODULUS = 65521.0


def reduce_mod(values):
    quotient = jnp.floor(values / MODULUS)
    leftover = values - quotient * MODULUS
    leftover = jnp.where(leftover < 0, leftover + MODULUS, leftover)
    return jnp.where(leftover >= MODULUS, leftover - MODULUS, leftover)


def split_digits(values):
    high_digit = jnp.floor(values / 256.0)
    return high_digit, values - 256.0 * high_digit


def combine_parts(high_part, middle_part, low_part):
    return reduce_mod(15.0 * reduce_mod(high_part) + reduce_mod(256.0 * reduce_mod(middle_part)) + reduce_mod(low_part))


def poly_product(left_side, right_side):
    span_width = left_side.shape[-1]
    left_high, left_low = split_digits(left_side)
    right_high, right_low = split_digits(right_side)
    stacked_left = jnp.concatenate([left_high, left_low], 1).astype(jnp.float32)
    stacked_right = jnp.concatenate([right_high, right_low], 2).astype(jnp.float32)
    products = jnp.einsum('kmj,kjn->kmn', stacked_left, stacked_right, precision=lax.Precision.HIGHEST)
    return combine_parts(products[:, :span_width, :span_width],
                         products[:, :span_width, span_width:] + products[:, span_width:, :span_width],
                         products[:, span_width:, span_width:])


def sigma_update(projections):
    span_width = projections[0].shape[0]
    term_count = len(projections) + 1
    identity = jnp.eye(span_width, dtype=jnp.float32)[None]
    polynomial = jnp.concatenate([identity, jnp.zeros((term_count - 1, span_width, span_width), jnp.float32)], 0)
    for step_index in range(1, term_count):
        known_terms = jnp.stack([projections[step_index - 1 - shift] for shift in range(step_index)])
        discrepancy = reduce_mod(jnp.sum(poly_product(polynomial[:step_index], known_terms), 0))
        scaled = poly_product(jnp.broadcast_to(discrepancy, polynomial.shape), polynomial)
        shifted = jnp.concatenate([jnp.zeros((1, span_width, span_width), jnp.float32), polynomial[:-1]], 0)
        polynomial = reduce_mod(shifted - scaled)
    return polynomial


def reference(tile_entries, tile_rows, tile_cols, tile_count, block_x, block_y):
    span_width = block_y.shape[0]
    tile_len = TILE_SIZE
    col_ids = jnp.arange(N_COL, dtype=jnp.int32)[:, None]
    global_cols = ((tile_cols // PIECE_BLOCKS) * ROW_BLOCKS + col_ids * PIECE_BLOCKS + tile_cols % PIECE_BLOCKS).astype(jnp.int32)
    live_slots = (jnp.arange(SLOTS, dtype=jnp.int32)[None, None, :] < tile_count[:, :, None]).astype(jnp.float32)
    onehot = (tile_rows[:, :, None, :] == jnp.arange(ROW_BLOCKS, dtype=jnp.int32)[None, None, :, None]).astype(jnp.float32)
    onehot = onehot * live_slots[:, :, None, :]

    def multiply(vector):
        high_v, low_v = split_digits(vector)
        v_digits = jnp.concatenate([high_v, low_v], 0).reshape(2 * span_width, ALL_BLOCKS, tile_len)

        def one_group(group_data):
            entries_group, group_cols, onehot_group = group_data
            high_a, low_a = split_digits(entries_group)
            a_digits = jnp.stack([high_a, low_a], 2)
            picked = v_digits[:, group_cols]
            products = jnp.einsum('nctk,ctdik->ctdni', picked, a_digits, precision=lax.Precision.HIGHEST)
            residues = combine_parts(products[:, :, 0, :span_width],
                                     products[:, :, 0, span_width:] + products[:, :, 1, :span_width],
                                     products[:, :, 1, span_width:])
            summed = reduce_mod(jnp.einsum('cbt,ctwi->cwbi', onehot_group, residues, precision=lax.Precision.HIGHEST))
            return reduce_mod(jnp.sum(summed, 0)).reshape(span_width, ROW_BLOCKS * tile_len)

        groups = lax.map(one_group, (tile_entries, global_cols, onehot))
        return jnp.transpose(groups, (1, 0, 2)).reshape(span_width, MATRIX_ORDER)

    def project(vector):
        high_x, low_x = split_digits(block_x)
        high_v, low_v = split_digits(vector)
        x_digits = jnp.concatenate([high_x, low_x], 0).reshape(2 * span_width, ALL_BLOCKS, tile_len)
        v_digits = jnp.concatenate([high_v, low_v], 0).reshape(2 * span_width, ALL_BLOCKS, tile_len)
        products = jnp.einsum('mbk,nbk->bmn', x_digits, v_digits, precision=lax.Precision.HIGHEST)
        residues = combine_parts(products[:, :span_width, :span_width],
                                 products[:, :span_width, span_width:] + products[:, span_width:, :span_width],
                                 products[:, span_width:, span_width:])
        residues = residues.reshape(N_ROW, N_COL, PIECE_BLOCKS, span_width, span_width)
        residues = reduce_mod(jnp.sum(residues, 2))
        residues = reduce_mod(jnp.sum(residues, 1))
        return reduce_mod(jnp.sum(residues, 0))

    vector = block_y
    projections = []
    for step_index in range(STEP_COUNT):
        vector = multiply(vector)
        projections.append(project(vector))
    polynomial = sigma_update(projections)
    return polynomial[:STEP_COUNT] / MODULUS, vector / MODULUS
```

```python
import functools

import jax
import jax.numpy as jnp
from jax import lax
from jax.experimental import pallas as pl
from jax.experimental.pallas import tpu as pltpu
from jax.sharding import PartitionSpec as P

STEP_COUNT = 3
MODULUS = 65521.0
INVERSE = 1.0 / 65521.0
MESH = pl.DeviceIdType.MESH
NX, NYL, NYH, NZ = 4, 4, 2, 8
F32, I32, BF16 = jnp.float32, jnp.int32, jnp.bfloat16


def reduce_mod(values):
    leftover = values - jnp.floor(values * INVERSE) * MODULUS
    leftover = jnp.where(leftover < 0, leftover + MODULUS, leftover)
    return jnp.where(leftover >= MODULUS, leftover - MODULUS, leftover)


def split_digits(values):
    high_digit = jnp.floor(values * (1.0 / 256.0))
    return (high_digit, values - 256.0 * high_digit)


def fold(values):
    high = values >> 16
    return (high << 4) - high + (values & 65535)


def times15(values):
    return (values << 4) - values


def kernel(
    order_ref, last_ref, entries_ref, x_ref, y_ref, c_ref, v_ref,
    ent, adig, xdig, gat, vdig, prods, part, lbuf, sbuf, ybuf, ysrc, vbuf, cloc, chalf, crecv, axb, ayb, azb,
    ent_sem, ys, yr, xs, xr, rs, rr, bs, br, ls, lr, hs, hr, ps, pr, cs, cr, axs, axr, ays, ayr, azs, azr,
):
    row, col = lax.axis_index("row"), lax.axis_index("col")
    core, yl, px = row % 2, (row // 2) % NYL, row // (2 * NYL)
    yh, pz = col // NZ, col % NZ
    step_r = 1 - 2 * core

    def rid(ax, ay, ac):
        return (((ax + 2 * NX) % NX) * NYL + (ay + 2 * NYL) % NYL) * 2 + ac

    def dev_x(d):
        return (rid(px + d, yl, core), col)

    def dev_y(d):
        whole = (yh * NYL + yl + d) % (NYL * NYH)
        return (rid(px, whole % NYL, core), (whole // NYL) * NZ + pz)

    def dev_z(d):
        return (row, yh * NZ + (pz + d + 2 * NZ) % NZ)

    sibling = (rid(px, yl, 1 - core), col)

    def remote(src, dst, ssem, rsem, dev):
        return pltpu.make_async_remote_copy(
            src_ref=src, dst_ref=dst, send_sem=ssem, recv_sem=rsem, device_id=dev, device_id_type=MESH
        )

    tile_total = ent.shape[0]
    chunk = 8

    def entry_copy(n):
        where = pl.ds(n * chunk, chunk)
        return pltpu.make_async_copy(entries_ref.at[where], ent.at[where], ent_sem.at[n])

    for n in range(tile_total // chunk):
        entry_copy(n).start()

    barrier = pltpu.get_barrier_semaphore()
    partners = [dev_x(d) for d in range(1, NX)] + [dev_y(d) for d in range(1, 8)]
    partners += [dev_z(d) for d in range(1, NZ)] + [sibling]
    for partner in partners:
        pl.semaphore_signal(barrier, inc=1, device_id=partner, device_id_type=MESH)

    high_x, low_x = split_digits(x_ref[...])
    xdig[0:64, :] = high_x.astype(BF16)
    xdig[64:128, :] = low_x.astype(BF16)
    vbuf[0] = y_ref[...]
    pl.semaphore_wait(barrier, len(partners))

    def gather(i, between):
        own = vbuf.at[i]
        sends = []

        def send(src, dst, ssem, rsem, dev):
            copy = remote(src, dst, ssem, rsem, dev)
            copy.start()
            sends.append(copy)

        def piece(r):
            return gat.at[i, r]

        def arrive(r, rsem):
            remote(piece(r), piece(r), bs.at[i, 0], rsem, sibling).wait_recv()

        def both_x(src, r, d):
            send(src, piece(r), xs.at[i, d, 0], xr.at[i, d, 0], dev_x(1))
            send(src, piece(r), xs.at[i, d, 1], xr.at[i, d, 1], dev_x(-1))

        def to_sibling(src, r, n):
            send(src, piece(r), bs.at[i, n], br.at[i, n], sibling)

        for d in range(1, NYL):
            target = (rid(px, yl + d, core), col)
            send(own, piece(row), ys.at[i, d - 1], yr.at[i, d - 1], target)
        both_x(own, row, 0)
        to_sibling(own, row, 0)
        gat[i, row] = vbuf[i]
        between(0)

        def relay(d):
            near = rid(px - step_r, yl - d, core)
            arrive(near, xr.at[i, d, core])
            send(piece(near), piece(near), rs.at[i, d], rr.at[i, d], dev_x(step_r))
            to_sibling(piece(near), near, 4 + d)

        for d in range(1, NYL):
            r = rid(px, yl - d, core)
            arrive(r, yr.at[i, d - 1])
            both_x(piece(r), r, d)
            to_sibling(piece(r), r, d)
            relay(d - 1)
            between(d)
        relay(NYL - 1)
        for d in range(NYL):
            other = rid(px + step_r, yl - d, core)
            arrive(other, xr.at[i, d, 1 - core])
            to_sibling(piece(other), other, 8 + d)
            far = rid(px + 2, yl - d, core)
            arrive(far, rr.at[i, d])
            to_sibling(piece(far), far, 12 + d)
        for n in range(16):
            shift = (0, step_r, -step_r, 2)[n // 4]
            arrive(rid(px + shift, yl - n % 4, 1 - core), br.at[i, n])
        for copy in sends:
            copy.wait_send()

    def make_digits(n):
        @pl.loop(n * chunk, (n + 1) * chunk)
        def _(t):
            high, low = split_digits(ent[t].T)
            adig[t, 0:128, :] = high.astype(BF16)
            adig[t, 128:256, :] = low.astype(BF16)

    def nothing(stage):
        del stage

    def first_between(stage):
        for n in (2 * stage, 2 * stage + 1):
            entry_copy(n).wait()
            make_digits(n)

    def multiply(i):
        @pl.loop(0, 32)
        def _(r):
            high, low = split_digits(gat[i, r])
            for j in range(2):
                vdig[2 * r + j, 0:64, :] = high[:, j * 128 : (j + 1) * 128].astype(BF16)
                vdig[2 * r + j, 64:128, :] = low[:, j * 128 : (j + 1) * 128].astype(BF16)

        blank = jnp.zeros((64, 128), BF16)
        width = 4

        def body(n, total):
            for u in range(width):
                j = n * width + u
                digits = vdig[order_ref[1, j]]
                high, low = digits[0:64], digits[64:128]
                left = jnp.concatenate(
                    [
                        jnp.concatenate([low, high], 1),
                        jnp.concatenate([high, blank], 1),
                        jnp.concatenate([blank, low], 1),
                    ],
                    0,
                )
                product = jnp.dot(left, adig[order_ref[0, j]], preferred_element_type=F32)
                total = (total & order_ref[2, j]) + product.astype(I32)
                prods[j] = total
            return total

        lax.fori_loop(0, tile_total // width, body, jnp.zeros((192, 128), I32))

    def slot_of(z, q):
        return (yh if q else 1 - yh) * NZ + (z + 2 * NZ) % NZ

    def fill(slot):
        for j in range(2):
            b = 2 * slot + j
            sums = prods[last_ref[0, b]] & last_ref[1, b]
            total = times15(fold(sums[64:128])) + (fold(sums[0:64]) << 8) + sums[128:192]
            part[slot, :, j * 128 : (j + 1) * 128] = reduce_mod(fold(total).astype(F32))

    def reduce(i):
        sends = []

        def long_copy(src, k, q):
            return remote(src, lbuf.at[i, k, q], ls.at[i, k, q], lr.at[i, k, q], dev_z(step_r))

        def short_copy(src, k, q):
            return remote(src, sbuf.at[i, k, q], hs.at[i, k, q], hr.at[i, k, q], dev_z(-step_r))

        def start(copy):
            copy.start()
            sends.append(copy)

        for q in range(2):
            slot = slot_of(pz + 4, q)
            fill(slot)
            start(long_copy(part.at[slot], 0, q))
            slot = slot_of(pz - 3 * step_r, q)
            fill(slot)
            start(short_copy(part.at[slot], 0, q))
        for k in range(3):
            for q in range(2):
                slot = slot_of(pz + (3 - k) * step_r, q)
                fill(slot)
                long_copy(part.at[slot], k, q).wait_recv()
                lbuf[i, k, q] = lbuf[i, k, q] + part[slot]
                start(long_copy(lbuf.at[i, k, q], k + 1, q))
                if k < 2:
                    slot = slot_of(pz - (2 - k) * step_r, q)
                    fill(slot)
                    short_copy(part.at[slot], k, q).wait_recv()
                    sbuf[i, k, q] = sbuf[i, k, q] + part[slot]
                    start(short_copy(sbuf.at[i, k, q], k + 1, q))
        swap = remote(ysrc.at[i], ybuf.at[i], ps.at[i], pr.at[i], dev_y(4))
        for q in range(2):
            slot = slot_of(pz, q)
            fill(slot)
            short_copy(part.at[slot], 2, q).wait_recv()
            long_copy(part.at[slot], 3, q).wait_recv()
            whole = lbuf[i, 3, q] + sbuf[i, 2, q] + part[slot]
            if q == 0:
                ysrc[i] = whole
                swap.start()
        swap.wait_recv()
        vbuf[i + 1] = reduce_mod(whole + ybuf[i])
        for copy in sends:
            copy.wait_send()
        swap.wait_send()

    def project(i):
        high, low = split_digits(vbuf[i + 1])
        digits = jnp.concatenate([high.astype(BF16), low.astype(BF16)], 0)
        products = lax.dot_general(
            xdig[...], digits, (((1,), (1,)), ((), ())), preferred_element_type=F32
        ).astype(I32)
        upper, lower = products[0:64], pltpu.roll(products[64:128], 64, 1)
        left_half = lax.broadcasted_iota(I32, (64, 128), 1) < 64
        mixed = jnp.where(left_half, times15(fold(upper)) + lower, fold(upper + lower) << 8)
        residues = reduce_mod(fold(mixed + pltpu.roll(mixed, 64, 1)).astype(F32))
        cloc[i] = jnp.where(left_half[0:32], residues[0:32], residues[32:64])

    gather(0, first_between)
    multiply(0)
    reduce(0)
    project(0)

    def later(i, carry):
        gather(i, nothing)
        multiply(i)
        reduce(i)
        project(i)
        return carry

    lax.fori_loop(1, STEP_COUNT, later, 0)
    v_ref[...] = vbuf[STEP_COUNT]

    halves = [remote(cloc.at[:, pl.ds(16 * (1 - core), 16)], crecv, cs.at[0], cr.at[0], sibling)]
    halves[0].start()
    halves[0].wait_recv()
    chalf[0] = cloc[:, pl.ds(16 * core, 16)] + crecv[...]

    def exchange(k, count, landing, ssem, rsem, dev):
        copies = []
        for d in range(1, count):
            copies.append(remote(chalf.at[k], landing.at[d - 1], ssem.at[d - 1], rsem.at[d - 1], dev(d)))
            copies[-1].start()
        total = chalf[k]
        for d in range(1, count):
            copies[d - 1].wait_recv()
            total = total + landing[d - 1]
        chalf[k + 1] = total if k == 0 else reduce_mod(total)
        halves.extend(copies)

    exchange(0, NX, axb, axs, axr, dev_x)
    exchange(1, NYL * NYH, ayb, ays, ayr, dev_y)
    exchange(2, NZ, azb, azs, azr, dev_z)
    mine = pl.ds(16 * core, 16)
    swap = remote(chalf.at[3], c_ref.at[:, mine], cs.at[1], cr.at[1], sibling)
    swap.start()
    c_ref[:, mine] = chalf[3]
    swap.wait_recv()
    swap.wait_send()
    for copy in halves:
        copy.wait_send()


def combine_parts(high_part, middle_part, low_part):
    return reduce_mod(
        15.0 * reduce_mod(high_part)
        + reduce_mod(256.0 * reduce_mod(middle_part))
        + reduce_mod(low_part)
    )


def poly_product(left_side, right_side):
    span_width = left_side.shape[-1]
    left_high, left_low = split_digits(left_side)
    right_high, right_low = split_digits(right_side)
    stacked_left = jnp.concatenate([left_high, left_low], 1).astype(BF16)
    stacked_right = jnp.concatenate([right_high, right_low], 2).astype(BF16)
    products = jnp.einsum("kmj,kjn->kmn", stacked_left, stacked_right, preferred_element_type=F32)
    return combine_parts(
        products[:, :span_width, :span_width],
        products[:, :span_width, span_width:] + products[:, span_width:, :span_width],
        products[:, span_width:, span_width:],
    )


def sigma_update(projections):
    span_width = projections[0].shape[0]
    term_count = len(projections) + 1
    identity = jnp.eye(span_width, dtype=F32)[None]
    polynomial = jnp.concatenate(
        [identity, jnp.zeros((term_count - 1, span_width, span_width), F32)], 0
    )
    for step_index in range(1, term_count):
        known_terms = jnp.stack(
            [projections[step_index - 1 - shift] for shift in range(step_index)]
        )
        discrepancy = reduce_mod(jnp.sum(poly_product(polynomial[:step_index], known_terms), 0))
        scaled = poly_product(jnp.broadcast_to(discrepancy, polynomial.shape), polynomial)
        shifted = jnp.concatenate(
            [jnp.zeros((1, span_width, span_width), F32), polynomial[:-1]], 0
        )
        polynomial = reduce_mod(shifted - scaled)
    return polynomial


def local(tile_entries, tile_rows, tile_cols, tile_count, block_x, block_y):
    entries = tile_entries[0, 0]
    slots = entries.shape[0]
    index = jnp.arange(slots, dtype=I32)
    keys = jnp.where(index < tile_count[0, 0], tile_rows[0, 0], 32)
    before = (keys[None, :] < keys[:, None]) | ((keys[None, :] == keys[:, None]) & (index[None, :] < index[:, None]))
    rank = jnp.sum(before.astype(I32), 1)
    chosen = (rank[None, :] == index[:, None]).astype(I32)
    order = jnp.sum(chosen * index[None, :], 1)
    columns = jnp.sum(chosen * tile_cols[0, 0][None, :], 1)
    sorted_keys = jnp.sum(chosen * keys[None, :], 1)
    same = jnp.concatenate([jnp.zeros((1,), jnp.bool_), sorted_keys[1:] == sorted_keys[:-1]])
    order_table = jnp.stack([order, columns, -same.astype(I32)])
    blocks = jnp.arange(32, dtype=I32)
    below = jnp.sum((keys[None, :] <= blocks[:, None]).astype(I32), 1)
    found = jnp.any(keys[None, :] == blocks[:, None], 1)
    last_table = jnp.stack([jnp.maximum(below - 1, 0), -found.astype(I32)])

    vmem = pl.BlockSpec(memory_space=pltpu.VMEM)
    smem = pl.BlockSpec(memory_space=pltpu.SMEM)
    steps = STEP_COUNT
    dma = pltpu.SemaphoreType.DMA
    projections, vector = pl.pallas_call(
        kernel,
        out_shape=(
            jax.ShapeDtypeStruct((steps, 32, 128), F32),
            jax.ShapeDtypeStruct((64, 256), F32),
        ),
        in_specs=[smem, smem, pl.BlockSpec(memory_space=pl.ANY), vmem, vmem],
        out_specs=(vmem, vmem),
        scratch_shapes=[
            pltpu.VMEM((slots, 128, 128), F32),
            pltpu.VMEM((slots, 256, 128), BF16),
            pltpu.VMEM((128, 256), BF16),
            pltpu.VMEM((steps, 32, 64, 256), F32),
            pltpu.VMEM((64, 128, 128), BF16),
            pltpu.VMEM((slots, 192, 128), I32),
            pltpu.VMEM((16, 64, 256), F32),
            pltpu.VMEM((steps, 4, 2, 64, 256), F32),
            pltpu.VMEM((steps, 3, 2, 64, 256), F32),
            pltpu.VMEM((steps, 64, 256), F32),
            pltpu.VMEM((steps, 64, 256), F32),
            pltpu.VMEM((steps + 1, 64, 256), F32),
            pltpu.VMEM((steps, 32, 128), F32),
            pltpu.VMEM((4, steps, 16, 128), F32),
            pltpu.VMEM((steps, 16, 128), F32),
            pltpu.VMEM((NX - 1, steps, 16, 128), F32),
            pltpu.VMEM((7, steps, 16, 128), F32),
            pltpu.VMEM((7, steps, 16, 128), F32),
            dma((8,)),
            dma((steps, 3)), dma((steps, 3)),
            dma((steps, 4, 2)), dma((steps, 4, 2)),
            dma((steps, 4)), dma((steps, 4)),
            dma((steps, 16)), dma((steps, 16)),
            dma((steps, 4, 2)), dma((steps, 4, 2)),
            dma((steps, 3, 2)), dma((steps, 3, 2)),
            dma((steps,)), dma((steps,)),
            dma((2,)), dma((2,)),
            dma((3,)), dma((3,)),
            dma((7,)), dma((7,)),
            dma((7,)), dma((7,)),
        ],
        compiler_params=pltpu.CompilerParams(
            collective_id=0, has_side_effects=True, vmem_limit_bytes=56 * 1024 * 1024
        ),
    )(order_table, last_table, entries, block_x, block_y)
    projections = jnp.concatenate([projections[:, :, :64], projections[:, :, 64:]], 1)
    polynomial = sigma_update([projections[n] for n in range(steps)])
    return (polynomial[:-1] / MODULUS, vector / MODULUS)


def solution(mesh):
    placed = (
        P("row", "col", None, None, None),
        P("row", "col", None),
        P("row", "col", None),
        P("row", "col"),
        P(None, ("row", "col")),
        P(None, ("row", "col")),
    )
    return jax.shard_map(
        local, mesh=mesh, in_specs=placed, out_specs=(P(), P(None, ("row", "col"))), check_vma=False
    )
```

```python
import functools

import jax
import jax.numpy as jnp
from jax import lax
from jax.experimental import pallas as pl
from jax.experimental.pallas import tpu as pltpu
from jax.sharding import PartitionSpec as P

STEP_COUNT = 3
MODULUS = 65521.0
INVERSE = 1.0 / 65521.0
MESH = pl.DeviceIdType.MESH
NX, NYL, NYH, NZ = 4, 4, 2, 8
F32, I32, BF16 = jnp.float32, jnp.int32, jnp.bfloat16


def reduce_mod(values):
    leftover = values - jnp.floor(values * INVERSE) * MODULUS
    leftover = jnp.where(leftover < 0, leftover + MODULUS, leftover)
    return jnp.where(leftover >= MODULUS, leftover - MODULUS, leftover)


def split_digits(values):
    high_digit = jnp.floor(values * (1.0 / 256.0))
    return (high_digit, values - 256.0 * high_digit)


def fold(values):
    high = values >> 16
    return (high << 4) - high + (values & 65535)


def times15(values):
    return (values << 4) - values


def kernel(
    order_ref, last_ref, entries_ref, x_ref, y_ref, c_ref, v_ref,
    ent, adig, xdig, gat, vdig, prods, part, lbuf, sbuf, ybuf, ysrc, vbuf, xall, cloc, chalf, crecv, axb, ayb, azb, cfull,
    ent_sem, ys, yr, xs, xr, rs, rr, bs, br, ls, lr, hs, hr, ps, pr, qs, qr, cs, cr, axs, axr, ays, ayr, azs, azr,
):
    row, col = lax.axis_index("row"), lax.axis_index("col")
    core, yl, px = row % 2, (row // 2) % NYL, row // (2 * NYL)
    yh, pz = col // NZ, col % NZ
    step_r = 1 - 2 * core

    def rid(ax, ay, ac):
        return (((ax + 2 * NX) % NX) * NYL + (ay + 2 * NYL) % NYL) * 2 + ac

    def dev_x(d):
        return (rid(px + d, yl, core), col)

    def dev_y(d):
        whole = (yh * NYL + yl + d) % (NYL * NYH)
        return (rid(px, whole % NYL, core), (whole // NYL) * NZ + pz)

    def dev_z(d):
        return (row, yh * NZ + (pz + d + 2 * NZ) % NZ)

    sibling = (rid(px, yl, 1 - core), col)

    def remote(src, dst, ssem, rsem, dev):
        return pltpu.make_async_remote_copy(
            src_ref=src, dst_ref=dst, send_sem=ssem, recv_sem=rsem, device_id=dev, device_id_type=MESH
        )

    tile_total = ent.shape[0]
    chunk = 8

    def entry_copy(n):
        where = pl.ds(n * chunk, chunk)
        return pltpu.make_async_copy(entries_ref.at[where], ent.at[where], ent_sem.at[n])

    for n in range(tile_total // chunk):
        entry_copy(n).start()

    barrier = pltpu.get_barrier_semaphore()
    partners = [dev_x(d) for d in range(1, NX)] + [dev_y(d) for d in range(1, 8)]
    partners += [dev_z(d) for d in range(1, NZ)] + [sibling]
    for partner in partners:
        pl.semaphore_signal(barrier, inc=1, device_id=partner, device_id_type=MESH)

    high_x, low_x = split_digits(x_ref[...])
    xdig[0:64, :] = high_x.astype(BF16)
    xdig[64:128, :] = low_x.astype(BF16)
    vbuf[0] = y_ref[...]
    pl.semaphore_wait(barrier, len(partners))

    def gather(i, between):
        own = vbuf.at[i]
        sends = []

        def send(src, dst, ssem, rsem, dev):
            copy = remote(src, dst, ssem, rsem, dev)
            copy.start()
            sends.append(copy)

        def piece(r):
            return gat.at[i, r]

        def arrive(r, rsem):
            remote(piece(r), piece(r), bs.at[i, 0], rsem, sibling).wait_recv()

        def both_x(src, r, d):
            send(src, piece(r), xs.at[i, d, 0], xr.at[i, d, 0], dev_x(1))
            send(src, piece(r), xs.at[i, d, 1], xr.at[i, d, 1], dev_x(-1))

        def to_sibling(src, r, n):
            send(src, piece(r), bs.at[i, n], br.at[i, n], sibling)

        for d in range(1, NYL):
            target = (rid(px, yl + d, core), col)
            send(own, piece(row), ys.at[i, d - 1], yr.at[i, d - 1], target)
        both_x(own, row, 0)
        to_sibling(own, row, 0)
        gat[i, row] = vbuf[i]
        between(0)

        def relay(d):
            near = rid(px - step_r, yl - d, core)
            arrive(near, xr.at[i, d, core])
            send(piece(near), piece(near), rs.at[i, d], rr.at[i, d], dev_x(step_r))
            to_sibling(piece(near), near, 4 + d)

        for d in range(1, NYL):
            r = rid(px, yl - d, core)
            arrive(r, yr.at[i, d - 1])
            both_x(piece(r), r, d)
            to_sibling(piece(r), r, d)
            relay(d - 1)
            between(d)
        relay(NYL - 1)
        for d in range(NYL):
            other = rid(px + step_r, yl - d, core)
            arrive(other, xr.at[i, d, 1 - core])
            to_sibling(piece(other), other, 8 + d)
            far = rid(px + 2, yl - d, core)
            arrive(far, rr.at[i, d])
            to_sibling(piece(far), far, 12 + d)
        for n in range(16):
            shift = (0, step_r, -step_r, 2)[n // 4]
            arrive(rid(px + shift, yl - n % 4, 1 - core), br.at[i, n])
        for copy in sends:
            copy.wait_send()

    def make_digits(n):
        @pl.loop(n * chunk, (n + 1) * chunk)
        def _(t):
            high, low = split_digits(ent[t].T)
            adig[t, 0:128, :] = high.astype(BF16)
            adig[t, 128:256, :] = low.astype(BF16)

    def nothing(stage):
        del stage

    def first_between(stage):
        for n in (2 * stage, 2 * stage + 1):
            entry_copy(n).wait()
            make_digits(n)

    def multiply(i):
        @pl.loop(0, 32)
        def _(r):
            high, low = split_digits(gat[i, r])
            for j in range(2):
                vdig[2 * r + j, 0:64, :] = high[:, j * 128 : (j + 1) * 128].astype(BF16)
                vdig[2 * r + j, 64:128, :] = low[:, j * 128 : (j + 1) * 128].astype(BF16)

        blank = jnp.zeros((64, 128), BF16)
        width = 4

        def body(n, total):
            for u in range(width):
                j = n * width + u
                digits = vdig[order_ref[1, j]]
                high, low = digits[0:64], digits[64:128]
                left = jnp.concatenate(
                    [
                        jnp.concatenate([low, high], 1),
                        jnp.concatenate([high, blank], 1),
                        jnp.concatenate([blank, low], 1),
                    ],
                    0,
                )
                product = jnp.dot(left, adig[order_ref[0, j]], preferred_element_type=F32)
                total = (total & order_ref[2, j]) + product.astype(I32)
                prods[j] = total
            return total

        lax.fori_loop(0, tile_total // width, body, jnp.zeros((192, 128), I32))

    def slot_of(z, q):
        return (yh if q else 1 - yh) * NZ + (z + 2 * NZ) % NZ

    def fill(slot):
        for j in range(2):
            b = 2 * slot + j
            sums = prods[last_ref[0, b]] & last_ref[1, b]
            total = times15(fold(sums[64:128])) + (fold(sums[0:64]) << 8) + sums[128:192]
            part[slot, :, j * 128 : (j + 1) * 128] = reduce_mod(fold(total).astype(F32))

    def reduce(i, between):
        sends = []

        def long_copy(src, k, q):
            return remote(src, lbuf.at[i, k, q], ls.at[i, k, q], lr.at[i, k, q], dev_z(step_r))

        def short_copy(src, k, q):
            return remote(src, sbuf.at[i, k, q], hs.at[i, k, q], hr.at[i, k, q], dev_z(-step_r))

        def start(copy):
            copy.start()
            sends.append(copy)

        for q in range(2):
            slot = slot_of(pz + 4, q)
            fill(slot)
            start(long_copy(part.at[slot], 0, q))
            slot = slot_of(pz - 3 * step_r, q)
            fill(slot)
            start(short_copy(part.at[slot], 0, q))
        for shift in (3, -2, 2, -1, 1, 0):
            for q in range(2):
                fill(slot_of(pz + shift * step_r, q))
        between(0)
        for k in range(3):
            for q in range(2):
                slot = slot_of(pz + (3 - k) * step_r, q)
                long_copy(part.at[slot], k, q).wait_recv()
                lbuf[i, k, q] = lbuf[i, k, q] + part[slot]
                start(long_copy(lbuf.at[i, k, q], k + 1, q))
                if k < 2:
                    slot = slot_of(pz - (2 - k) * step_r, q)
                    short_copy(part.at[slot], k, q).wait_recv()
                    sbuf[i, k, q] = sbuf[i, k, q] + part[slot]
                    start(short_copy(sbuf.at[i, k, q], k + 1, q))
            between(k + 1)
        swap = remote(ysrc.at[i], ybuf.at[i], ps.at[i], pr.at[i], dev_y(4))
        for q in range(2):
            slot = slot_of(pz, q)
            short_copy(part.at[slot], 2, q).wait_recv()
            long_copy(part.at[slot], 3, q).wait_recv()
            whole = lbuf[i, 3, q] + sbuf[i, 2, q] + part[slot]
            if q == 0:
                ysrc[i] = whole
                swap.start()
        between(4)
        swap.wait_recv()
        vbuf[i + 1] = reduce_mod(whole + ybuf[i])
        sends.append(swap)
        return sends

    left_half = lax.broadcasted_iota(I32, (64, 128), 1) < 64

    def quads(products):
        upper, lower = products[0:64], pltpu.roll(products[64:128], 64, 1)
        mixed = jnp.where(left_half, times15(fold(upper)) + lower, fold(upper + lower) << 8)
        return reduce_mod(fold(mixed + pltpu.roll(mixed, 64, 1)).astype(F32))

    def stacked(values):
        high, low = split_digits(values)
        return jnp.concatenate([high.astype(BF16), low.astype(BF16)], 0)

    def project(x_digits, values):
        return lax.dot_general(
            x_digits, stacked(values), (((1,), (1,)), ((), ())), preferred_element_type=F32
        ).astype(I32)

    def keep_terms(i, products):
        residues = quads(products)
        cloc[i] = jnp.where(left_half[0:32], residues[0:32], residues[32:64])

    mine = pl.ds(16 * core, 16)
    theirs = pl.ds(16 - 16 * core, 16)
    pending = []

    def sum_stages(i):
        first = remote(cloc.at[i, theirs], crecv.at[i], cs.at[i, 0], cr.at[i, 0], sibling)
        last = remote(chalf.at[i, 3], cfull.at[i, mine], cs.at[i, 1], cr.at[i, 1], sibling)

        def copies(k, count, landing, ssem, rsem, dev):
            return [
                remote(chalf.at[i, k], landing.at[i, d - 1], ssem.at[i, d - 1], rsem.at[i, d - 1], dev(d))
                for d in range(1, count)
            ]

        rounds = [
            (copies(0, NX, axb, axs, axr, dev_x), axb),
            (copies(1, NYL * NYH, ayb, ays, ayr, dev_y), ayb),
            (copies(2, NZ, azb, azs, azr, dev_z), azb),
        ]

        def begin(k):
            for copy in rounds[k][0]:
                copy.start()
            pending.extend(rounds[k][0])

        def finish(k):
            total = chalf[i, k]
            for d, copy in enumerate(rounds[k][0]):
                copy.wait_recv()
                total = total + rounds[k][1][i, d]
            chalf[i, k + 1] = total if k == 0 else reduce_mod(total)

        def stage(n):
            if n == 0:
                first.start()
                pending.append(first)
            elif n == 1:
                first.wait_recv()
                chalf[i, 0] = cloc[i, mine] + crecv[i]
                begin(0)
            elif n < 4:
                finish(n - 2)
                begin(n - 1)
            elif n == 4:
                finish(2)
                last.start()
                pending.append(last)
                cfull[i, mine] = chalf[i, 3]
            else:
                last.wait_recv()

        return stage

    def twice(i):
        packed = cfull[i]
        turned = pltpu.roll(packed, 64, 1)
        return jnp.concatenate(
            [jnp.where(left_half[0:32], packed, turned), jnp.where(left_half[0:32], turned, packed)], 0
        )

    def times(left, right):
        left_digits = stacked(left)[:, 0:64]
        high, low = split_digits(right)
        right_digits = jnp.where(left_half, high, low).astype(BF16)
        return quads(jnp.dot(left_digits, right_digits, preferred_element_type=F32).astype(I32))

    def send_x(source, where, k):
        copies = []
        for d in range(1, NZ):
            copies.append(remote(source, xall.at[where], qs.at[k, d], qr.at[k, d], dev_z(d)))
            copies[-1].start()
        pending.extend(copies)

    partner_col = (1 - yh) * NZ + pz
    x_swap = remote(x_ref, xall.at[col], qs.at[0, 0], qr.at[0, 0], dev_y(4))
    x_swap.start()
    pending.append(x_swap)
    send_x(x_ref, col, 0)
    xall[col] = x_ref[...]

    stages = [sum_stages(i) for i in range(STEP_COUNT)]

    gather(0, first_between)
    multiply(0)
    sends = reduce(0, nothing)
    remote(x_ref, xall.at[partner_col], qs.at[0, 0], qr.at[0, 0], dev_y(4)).wait_recv()

    def second_between(stage):
        if stage == 0:
            send_x(xall.at[partner_col], partner_col, 1)
            keep_terms(0, project(xdig[...], vbuf[1]))
        stages[0](stage)

    def second_reduce(stage):
        if stage == 0:
            stages[0](4)
        if stage == 1:
            stages[0](5)

    gather(1, second_between)
    multiply(1)
    for copy in sends:
        copy.wait_send()
    sends = reduce(1, second_reduce)

    def third_between(stage):
        if stage == 0:
            keep_terms(1, project(xdig[...], vbuf[2]))
        stages[1](stage)

    gather(2, third_between)
    stages[1](4)
    multiply(2)
    stages[1](5)
    for copy in sends:
        copy.wait_send()
    for k in range(2):
        for d in range(1, NZ):
            where = (yh if k == 0 else 1 - yh) * NZ + (pz - d + NZ) % NZ
            remote(x_ref, xall.at[where], qs.at[k, d], qr.at[k, d], dev_z(d)).wait_recv()

    known = {}

    def third_reduce(stage):
        if stage == 0:
            total = jnp.zeros((128, 128), I32)
            for slot in range(16):
                total = total + project(stacked(xall[slot]), part[slot])
            keep_terms(2, total)
            stages[2](0)
            first, second = twice(0), twice(1)
            known["zero"] = reduce_mod(-first)
            error = reduce_mod(times(known["zero"], second) + first)
            known["one"] = reduce_mod(known["zero"] - error)
            known["zero"] = reduce_mod(-times(error, known["zero"]))
            known["rest"] = times(known["one"], second) + first
            stages[2](1)
        else:
            stages[2](stage + 1)

    sends = reduce(2, third_reduce)
    v_ref[...] = vbuf[STEP_COUNT] / MODULUS
    error = reduce_mod(times(known["zero"], twice(2)) + known["rest"])
    c_ref[0] = (reduce_mod(-times(error, known["zero"])) / MODULUS)[:, 0:64]
    c_ref[1] = (reduce_mod(known["zero"] - times(error, known["one"])) / MODULUS)[:, 0:64]
    c_ref[2] = (reduce_mod(known["one"] - error) / MODULUS)[:, 0:64]
    for copy in sends + pending:
        copy.wait_send()


def local(tile_entries, tile_rows, tile_cols, tile_count, block_x, block_y):
    entries = tile_entries[0, 0]
    slots = entries.shape[0]
    index = jnp.arange(slots, dtype=I32)
    keys = jnp.where(index < tile_count[0, 0], tile_rows[0, 0], 32)
    before = (keys[None, :] < keys[:, None]) | ((keys[None, :] == keys[:, None]) & (index[None, :] < index[:, None]))
    rank = jnp.sum(before.astype(I32), 1)
    chosen = (rank[None, :] == index[:, None]).astype(I32)
    order = jnp.sum(chosen * index[None, :], 1)
    columns = jnp.sum(chosen * tile_cols[0, 0][None, :], 1)
    sorted_keys = jnp.sum(chosen * keys[None, :], 1)
    same = jnp.concatenate([jnp.zeros((1,), jnp.bool_), sorted_keys[1:] == sorted_keys[:-1]])
    order_table = jnp.stack([order, columns, -same.astype(I32)])
    blocks = jnp.arange(32, dtype=I32)
    below = jnp.sum((keys[None, :] <= blocks[:, None]).astype(I32), 1)
    found = jnp.any(keys[None, :] == blocks[:, None], 1)
    last_table = jnp.stack([jnp.maximum(below - 1, 0), -found.astype(I32)])

    vmem = pl.BlockSpec(memory_space=pltpu.VMEM)
    smem = pl.BlockSpec(memory_space=pltpu.SMEM)
    steps = STEP_COUNT
    dma = pltpu.SemaphoreType.DMA
    return pl.pallas_call(
        kernel,
        out_shape=(
            jax.ShapeDtypeStruct((steps, 64, 64), F32),
            jax.ShapeDtypeStruct((64, 256), F32),
        ),
        in_specs=[smem, smem, pl.BlockSpec(memory_space=pl.ANY), vmem, vmem],
        out_specs=(vmem, vmem),
        scratch_shapes=[
            pltpu.VMEM((slots, 128, 128), F32),
            pltpu.VMEM((slots, 256, 128), BF16),
            pltpu.VMEM((128, 256), BF16),
            pltpu.VMEM((steps, 32, 64, 256), F32),
            pltpu.VMEM((64, 128, 128), BF16),
            pltpu.VMEM((slots, 192, 128), I32),
            pltpu.VMEM((16, 64, 256), F32),
            pltpu.VMEM((steps, 4, 2, 64, 256), F32),
            pltpu.VMEM((steps, 3, 2, 64, 256), F32),
            pltpu.VMEM((steps, 64, 256), F32),
            pltpu.VMEM((steps, 64, 256), F32),
            pltpu.VMEM((steps + 1, 64, 256), F32),
            pltpu.VMEM((16, 64, 256), F32),
            pltpu.VMEM((steps, 32, 128), F32),
            pltpu.VMEM((steps, 4, 16, 128), F32),
            pltpu.VMEM((steps, 16, 128), F32),
            pltpu.VMEM((steps, NX - 1, 16, 128), F32),
            pltpu.VMEM((steps, 7, 16, 128), F32),
            pltpu.VMEM((steps, 7, 16, 128), F32),
            pltpu.VMEM((steps, 32, 128), F32),
            dma((8,)),
            dma((steps, 3)), dma((steps, 3)),
            dma((steps, 4, 2)), dma((steps, 4, 2)),
            dma((steps, 4)), dma((steps, 4)),
            dma((steps, 16)), dma((steps, 16)),
            dma((steps, 4, 2)), dma((steps, 4, 2)),
            dma((steps, 3, 2)), dma((steps, 3, 2)),
            dma((steps,)), dma((steps,)),
            dma((2, 8)), dma((2, 8)),
            dma((steps, 2)), dma((steps, 2)),
            dma((steps, 3)), dma((steps, 3)),
            dma((steps, 7)), dma((steps, 7)),
            dma((steps, 7)), dma((steps, 7)),
        ],
        compiler_params=pltpu.CompilerParams(
            collective_id=0, has_side_effects=True, vmem_limit_bytes=56 * 1024 * 1024
        ),
    )(order_table, last_table, entries, block_x, block_y)


def solution(mesh):
    placed = (
        P("row", "col", None, None, None),
        P("row", "col", None),
        P("row", "col", None),
        P("row", "col"),
        P(None, ("row", "col")),
        P(None, ("row", "col")),
    )
    return jax.shard_map(
        local, mesh=mesh, in_specs=placed, out_specs=(P(), P(None, ("row", "col"))), check_vma=False
    )
```

```python
import functools

import jax
import jax.numpy as jnp
from jax import lax
from jax.experimental import pallas as pl
from jax.experimental.pallas import tpu as pltpu
from jax.sharding import PartitionSpec as P

STEP_COUNT = 3
MODULUS = 65521.0
INVERSE = 1.0 / 65521.0
MESH = pl.DeviceIdType.MESH
NX, NYL, NYH, NZ = 4, 4, 2, 8
DIRECT = (0, 1, 2, 3)
F32, I32, BF16 = jnp.float32, jnp.int32, jnp.bfloat16


def reduce_mod(values):
    leftover = values - jnp.floor(values * INVERSE) * MODULUS
    leftover = jnp.where(leftover < 0, leftover + MODULUS, leftover)
    return jnp.where(leftover >= MODULUS, leftover - MODULUS, leftover)


def split_digits(values):
    high_digit = jnp.floor(values * (1.0 / 256.0))
    return (high_digit, values - 256.0 * high_digit)


def fold(values):
    high = values >> 16
    return (high << 4) - high + (values & 65535)


def times15(values):
    return (values << 4) - values


def kernel(
    rows_ref, cols_ref, count_ref, entries_ref, x_ref, y_ref, c_ref, v_ref,
    ent, adig, xdig, gat, vdig, prods, part, lbuf, sbuf, ybuf, ysrc, vbuf, xall, cloc, chalf, crecv, axb, ayb, azb, cfull, xall_digits, tables, table,
    table_sem, ent_sem, ys, yr, xs, xr, rs, rr, bs, br, ls, lr, hs, hr, ps, pr, qs, qr, cs, cr, axs, axr, ays, ayr, azs, azr,
):
    row, col = lax.axis_index("row"), lax.axis_index("col")
    core, yl, px = row % 2, (row // 2) % NYL, row // (2 * NYL)
    yh, pz = col // NZ, col % NZ
    step_r = 1 - 2 * core

    def rid(ax, ay, ac):
        return (((ax + 2 * NX) % NX) * NYL + (ay + 2 * NYL) % NYL) * 2 + ac

    def dev_x(d):
        return (rid(px + d, yl, core), col)

    def dev_y(d):
        whole = (yh * NYL + yl + d) % (NYL * NYH)
        return (rid(px, whole % NYL, core), (whole // NYL) * NZ + pz)

    def dev_z(d):
        return (row, yh * NZ + (pz + d + 2 * NZ) % NZ)

    sibling = (rid(px, yl, 1 - core), col)

    def remote(src, dst, ssem, rsem, dev):
        return pltpu.make_async_remote_copy(
            src_ref=src, dst_ref=dst, send_sem=ssem, recv_sem=rsem, device_id=dev, device_id_type=MESH
        )

    tile_total = ent.shape[0]
    chunk = 8

    def entry_copy(n):
        where = pl.ds(n * chunk, chunk)
        return pltpu.make_async_copy(entries_ref.at[where], ent.at[where], ent_sem.at[n])

    for n in range(tile_total // chunk):
        entry_copy(n).start()

    barrier = pltpu.get_barrier_semaphore()
    partners = [dev_x(d) for d in range(1, NX)] + [dev_y(d) for d in range(1, 8)]
    partners += [dev_z(d) for d in range(1, NZ)] + [sibling]
    for partner in partners:
        pl.semaphore_signal(barrier, inc=1, device_id=partner, device_id_type=MESH)

    high_x, low_x = split_digits(x_ref[...])
    xdig[0:64, :] = high_x.astype(BF16)
    xdig[64:128, :] = low_x.astype(BF16)
    vbuf[0] = y_ref[...]
    pl.semaphore_wait(barrier, len(partners))

    def gather(i, between):
        own = vbuf.at[i]
        sends = []

        def send(src, dst, ssem, rsem, dev):
            copy = remote(src, dst, ssem, rsem, dev)
            copy.start()
            sends.append(copy)

        def piece(r):
            return gat.at[i, r]

        def arrive(r, rsem):
            remote(piece(r), piece(r), bs.at[i, 0], rsem, sibling).wait_recv()

        def both_x(src, r, d):
            send(src, piece(r), xs.at[i, d, 0], xr.at[i, d, 0], dev_x(1))
            send(src, piece(r), xs.at[i, d, 1], xr.at[i, d, 1], dev_x(-1))
            if d in DIRECT:
                send(src, piece(r), rs.at[i, d], rr.at[i, d], dev_x(2))

        def to_sibling(src, r, n):
            send(src, piece(r), bs.at[i, n], br.at[i, n], sibling)

        for d in range(1, NYL):
            target = (rid(px, yl + d, core), col)
            send(own, piece(row), ys.at[i, d - 1], yr.at[i, d - 1], target)
        both_x(own, row, 0)
        to_sibling(own, row, 0)
        gat[i, row] = vbuf[i]
        between(0)

        def relay(d):
            near = rid(px - step_r, yl - d, core)
            arrive(near, xr.at[i, d, core])
            if d not in DIRECT:
                send(piece(near), piece(near), rs.at[i, d], rr.at[i, d], dev_x(step_r))
            to_sibling(piece(near), near, 4 + d)

        for d in range(1, NYL):
            r = rid(px, yl - d, core)
            arrive(r, yr.at[i, d - 1])
            both_x(piece(r), r, d)
            to_sibling(piece(r), r, d)
            relay(d - 1)
            between(d)
        relay(NYL - 1)
        for d in range(NYL):
            other = rid(px + step_r, yl - d, core)
            arrive(other, xr.at[i, d, 1 - core])
            to_sibling(piece(other), other, 8 + d)
            far = rid(px + 2, yl - d, core)
            arrive(far, rr.at[i, d])
            to_sibling(piece(far), far, 12 + d)
        for n in range(16):
            shift = (0, step_r, -step_r, 2)[n // 4]
            arrive(rid(px + shift, yl - n % 4, 1 - core), br.at[i, n])
        for copy in sends:
            copy.wait_send()

    def make_tables():
        shape = (tile_total, tile_total)
        down, across = lax.broadcasted_iota(I32, shape, 0), lax.broadcasted_iota(I32, shape, 1)

        def upright(flat):
            return jnp.sum(jnp.where(down == across, flat, 0), 1, keepdims=True)

        def add_up(values):
            return jnp.sum(values, 0, keepdims=True)

        tables[...] = jnp.zeros((8, 128), I32)
        live = across < count_ref[0, 0]
        flat_keys = jnp.where(live, jnp.broadcast_to(rows_ref[...], shape), 32)
        keys = upright(flat_keys)
        earlier = (flat_keys == keys) & (across < down)
        rank = jnp.sum(((flat_keys < keys) | earlier).astype(I32), 1, keepdims=True)
        repeated = jnp.max(earlier.astype(I32), 1, keepdims=True)
        chosen = rank == across
        columns = upright(jnp.broadcast_to(cols_ref[...], shape))
        tables[0:1, 0:64] = add_up(jnp.where(chosen, down, 0))
        tables[1:2, 0:64] = add_up(jnp.where(chosen, columns, 0))
        tables[2:3, 0:64] = add_up(jnp.where(chosen, -repeated, 0))
        tables[3:4, 0:64] = jnp.maximum(add_up((keys <= across).astype(I32)) - 1, 0)
        tables[4:5, 0:64] = -jnp.max((keys == across).astype(I32), 0, keepdims=True)
        return pltpu.make_async_copy(tables, table, table_sem)

    def make_digits(n):
        @pl.loop(n * chunk, (n + 1) * chunk)
        def _(t):
            high, low = split_digits(ent[t].T)
            adig[t, :, 0:128] = high.astype(BF16)
            adig[t, :, 128:256] = low.astype(BF16)

    def nothing(stage):
        del stage

    def first_between(stage):
        if stage == 0:
            moved = make_tables()
            moved.start()
            moved.wait()
        for n in (2 * stage, 2 * stage + 1):
            entry_copy(n).wait()
            make_digits(n)

    def multiply(i):
        @pl.loop(0, 32)
        def _(r):
            high, low = split_digits(gat[i, r])
            for j in range(2):
                vdig[2 * r + j, 0:64, :] = high[:, j * 128 : (j + 1) * 128].astype(BF16)
                vdig[2 * r + j, 64:128, :] = low[:, j * 128 : (j + 1) * 128].astype(BF16)

        width = 16

        def body(n, total):
            for u in range(width):
                j = n * width + u
                p = jnp.dot(vdig[table[1, j]], adig[table[0, j]], preferred_element_type=F32)
                middle = p[0:64, 128:256] + p[64:128, 0:128]
                product = jnp.concatenate([middle, p[0:64, 0:128], p[64:128, 128:256]], 0)
                total = (total & table[2, j]) + product.astype(I32)
                prods[j] = total
            return total

        lax.fori_loop(0, tile_total // width, body, jnp.zeros((192, 128), I32))

    def slot_of(z, q):
        return (yh if q else 1 - yh) * NZ + (z + 2 * NZ) % NZ

    def fill(slot):
        for j in range(2):
            b = 2 * slot + j
            sums = prods[table[3, b]] & table[4, b]
            total = times15(fold(sums[64:128])) + (fold(sums[0:64]) << 8) + sums[128:192]
            part[slot, :, j * 128 : (j + 1) * 128] = reduce_mod(fold(total).astype(F32))

    def reduce(i, between):
        sends = []

        def long_copy(src, k, q):
            return remote(src, lbuf.at[i, k, q], ls.at[i, k, q], lr.at[i, k, q], dev_z(step_r))

        def short_copy(src, k, q):
            return remote(src, sbuf.at[i, k, q], hs.at[i, k, q], hr.at[i, k, q], dev_z(-step_r))

        def start(copy):
            copy.start()
            sends.append(copy)

        def own(z, q):
            return part.at[slot_of(z, q // 2), pl.ds(32 * (q % 2), 32)]

        for q in range(4):
            if q % 2 == 0:
                fill(slot_of(pz + 4, q // 2))
            start(long_copy(own(pz + 4, q), 0, q))
            if q % 2 == 0:
                fill(slot_of(pz - 3 * step_r, q // 2))
            start(short_copy(own(pz - 3 * step_r, q), 0, q))
        for shift in (3, -2, 2, -1, 1, 0):
            for q in range(2):
                fill(slot_of(pz + shift * step_r, q))
        between(0)
        for k in range(3):
            for q in range(4):
                mine_here = own(pz + (3 - k) * step_r, q)
                long_copy(mine_here, k, q).wait_recv()
                lbuf[i, k, q] = lbuf[i, k, q] + mine_here[...]
                start(long_copy(lbuf.at[i, k, q], k + 1, q))
                if k < 2:
                    mine_here = own(pz - (2 - k) * step_r, q)
                    short_copy(mine_here, k, q).wait_recv()
                    sbuf[i, k, q] = sbuf[i, k, q] + mine_here[...]
                    start(short_copy(sbuf.at[i, k, q], k + 1, q))
            between(k + 1)
        swaps = []
        wholes = []
        for q in range(4):
            mine_here = own(pz, q)
            short_copy(mine_here, 2, q).wait_recv()
            long_copy(mine_here, 3, q).wait_recv()
            whole = lbuf[i, 3, q] + sbuf[i, 2, q] + mine_here[...]
            if q < 2:
                ysrc[i, q] = whole
                swaps.append(remote(ysrc.at[i, q], ybuf.at[i, q], ps.at[i, q], pr.at[i, q], dev_y(4)))
                swaps[-1].start()
            else:
                wholes.append(whole)
        between(4)
        for q in range(2):
            swaps[q].wait_recv()
            vbuf[i + 1, pl.ds(32 * q, 32)] = reduce_mod(wholes[q] + ybuf[i, q])
        sends.extend(swaps)
        return sends

    left_half = lax.broadcasted_iota(I32, (64, 128), 1) < 64

    def quads(products):
        upper, lower = products[0:64], pltpu.roll(products[64:128], 64, 1)
        mixed = jnp.where(left_half, times15(fold(upper)) + lower, fold(upper + lower) << 8)
        return reduce_mod(fold(mixed + pltpu.roll(mixed, 64, 1)).astype(F32))

    def stacked(values):
        high, low = split_digits(values)
        return jnp.concatenate([high.astype(BF16), low.astype(BF16)], 0)

    def project(x_digits, values):
        return lax.dot_general(
            x_digits, stacked(values), (((1,), (1,)), ((), ())), preferred_element_type=F32
        ).astype(I32)

    def keep_terms(i, products):
        residues = quads(products)
        cloc[i] = jnp.where(left_half[0:32], residues[0:32], residues[32:64])

    mine = pl.ds(16 * core, 16)
    theirs = pl.ds(16 - 16 * core, 16)
    pending = []

    def sum_stages(i):
        first = remote(cloc.at[i, theirs], crecv.at[i], cs.at[i, 0], cr.at[i, 0], sibling)
        last = remote(chalf.at[i, 3], cfull.at[i, mine], cs.at[i, 1], cr.at[i, 1], sibling)

        def copies(k, count, landing, ssem, rsem, dev):
            return [
                remote(chalf.at[i, k], landing.at[i, d - 1], ssem.at[i, d - 1], rsem.at[i, d - 1], dev(d))
                for d in range(1, count)
            ]

        rounds = [
            (copies(0, NX, axb, axs, axr, dev_x), axb),
            (copies(1, NYL * NYH, ayb, ays, ayr, dev_y), ayb),
            (copies(2, NZ, azb, azs, azr, dev_z), azb),
        ]

        def begin(k):
            for copy in rounds[k][0]:
                copy.start()
            pending.extend(rounds[k][0])

        def finish(k):
            total = chalf[i, k]
            for d, copy in enumerate(rounds[k][0]):
                copy.wait_recv()
                total = total + rounds[k][1][i, d]
            chalf[i, k + 1] = total if k == 0 else reduce_mod(total)

        def stage(n):
            if n == 0:
                first.start()
                pending.append(first)
            elif n == 1:
                first.wait_recv()
                chalf[i, 0] = cloc[i, mine] + crecv[i]
                begin(0)
            elif n < 4:
                finish(n - 2)
                begin(n - 1)
            elif n == 4:
                finish(2)
                last.start()
                pending.append(last)
                cfull[i, mine] = chalf[i, 3]
            else:
                last.wait_recv()

        return stage

    def twice(i):
        packed = cfull[i]
        turned = pltpu.roll(packed, 64, 1)
        return jnp.concatenate(
            [jnp.where(left_half[0:32], packed, turned), jnp.where(left_half[0:32], turned, packed)], 0
        )

    def times(left, right):
        left_digits = stacked(left)[:, 0:64]
        high, low = split_digits(right)
        right_digits = jnp.where(left_half, high, low).astype(BF16)
        return quads(jnp.dot(left_digits, right_digits, preferred_element_type=F32).astype(I32))

    def send_x(source, where, k):
        copies = []
        for d in range(1, NZ):
            copies.append(remote(source, xall.at[where], qs.at[k, d], qr.at[k, d], dev_z(d)))
            copies[-1].start()
        pending.extend(copies)

    partner_col = (1 - yh) * NZ + pz
    x_swap = remote(x_ref, xall.at[col], qs.at[0, 0], qr.at[0, 0], dev_y(4))
    x_swap.start()
    pending.append(x_swap)
    send_x(x_ref, col, 0)
    xall[col] = x_ref[...]

    stages = [sum_stages(i) for i in range(STEP_COUNT)]

    gather(0, first_between)
    multiply(0)
    sends = reduce(0, nothing)
    remote(x_ref, xall.at[partner_col], qs.at[0, 0], qr.at[0, 0], dev_y(4)).wait_recv()

    def second_between(stage):
        if stage == 0:
            send_x(xall.at[partner_col], partner_col, 1)
            keep_terms(0, project(xdig[...], vbuf[1]))
        stages[0](stage)

    def second_reduce(stage):
        if stage == 0:
            stages[0](4)
        if stage == 1:
            stages[0](5)

    gather(1, second_between)
    multiply(1)
    for copy in sends:
        copy.wait_send()
    sends = reduce(1, second_reduce)

    def receive_x():
        for k in range(2):
            for d in range(1, NZ):
                where = (yh if k == 0 else 1 - yh) * NZ + (pz - d + NZ) % NZ
                remote(x_ref, xall.at[where], qs.at[k, d], qr.at[k, d], dev_z(d)).wait_recv()

    def third_between(stage):
        if stage == 0:
            keep_terms(1, project(xdig[...], vbuf[2]))
            receive_x()
        for slot in range(4 * stage, 4 * stage + 4):
            xall_digits[slot] = stacked(xall[slot])
        stages[1](stage)

    gather(2, third_between)
    stages[1](4)
    multiply(2)
    stages[1](5)
    for copy in sends:
        copy.wait_send()
    known = {}

    def third_reduce(stage):
        if stage == 0:
            total = jnp.zeros((128, 128), I32)
            for slot in range(16):
                total = total + project(xall_digits[slot], part[slot])
            keep_terms(2, total)
            stages[2](0)
            first, second = twice(0), twice(1)
            known["zero"] = reduce_mod(-first)
            error = reduce_mod(times(known["zero"], second) + first)
            known["one"] = reduce_mod(known["zero"] - error)
            known["zero"] = reduce_mod(-times(error, known["zero"]))
            known["rest"] = times(known["one"], second) + first
            stages[2](1)
        else:
            stages[2](stage + 1)

    sends = reduce(2, third_reduce)
    v_ref[...] = vbuf[STEP_COUNT] / MODULUS
    error = reduce_mod(times(known["zero"], twice(2)) + known["rest"])
    c_ref[0] = (reduce_mod(-times(error, known["zero"])) / MODULUS)[:, 0:64]
    c_ref[1] = (reduce_mod(known["zero"] - times(error, known["one"])) / MODULUS)[:, 0:64]
    c_ref[2] = (reduce_mod(known["one"] - error) / MODULUS)[:, 0:64]
    for copy in sends + pending:
        copy.wait_send()


def local(tile_entries, tile_rows, tile_cols, tile_count, block_x, block_y):
    entries = tile_entries[0, 0]
    slots = entries.shape[0]
    vmem = pl.BlockSpec(memory_space=pltpu.VMEM)
    smem = pl.BlockSpec(memory_space=pltpu.SMEM)
    steps = STEP_COUNT
    dma = pltpu.SemaphoreType.DMA
    return pl.pallas_call(
        kernel,
        out_shape=(
            jax.ShapeDtypeStruct((steps, 64, 64), F32),
            jax.ShapeDtypeStruct((64, 256), F32),
        ),
        in_specs=[vmem, vmem, smem, pl.BlockSpec(memory_space=pl.ANY), vmem, vmem],
        out_specs=(vmem, vmem),
        scratch_shapes=[
            pltpu.VMEM((slots, 128, 128), F32),
            pltpu.VMEM((slots, 128, 256), BF16),
            pltpu.VMEM((128, 256), BF16),
            pltpu.VMEM((steps, 32, 64, 256), F32),
            pltpu.VMEM((64, 128, 128), BF16),
            pltpu.VMEM((slots, 192, 128), I32),
            pltpu.VMEM((16, 64, 256), F32),
            pltpu.VMEM((steps, 4, 4, 32, 256), F32),
            pltpu.VMEM((steps, 3, 4, 32, 256), F32),
            pltpu.VMEM((steps, 2, 32, 256), F32),
            pltpu.VMEM((steps, 2, 32, 256), F32),
            pltpu.VMEM((steps + 1, 64, 256), F32),
            pltpu.VMEM((16, 64, 256), F32),
            pltpu.VMEM((steps, 32, 128), F32),
            pltpu.VMEM((steps, 4, 16, 128), F32),
            pltpu.VMEM((steps, 16, 128), F32),
            pltpu.VMEM((steps, NX - 1, 16, 128), F32),
            pltpu.VMEM((steps, 7, 16, 128), F32),
            pltpu.VMEM((steps, 7, 16, 128), F32),
            pltpu.VMEM((steps, 32, 128), F32),
            pltpu.VMEM((16, 128, 256), BF16),
            pltpu.VMEM((8, 128), I32),
            pltpu.SMEM((8, 128), I32),
            dma(()),
            dma((8,)),
            dma((steps, 3)), dma((steps, 3)),
            dma((steps, 4, 2)), dma((steps, 4, 2)),
            dma((steps, 4)), dma((steps, 4)),
            dma((steps, 16)), dma((steps, 16)),
            dma((steps, 4, 4)), dma((steps, 4, 4)),
            dma((steps, 3, 4)), dma((steps, 3, 4)),
            dma((steps, 2)), dma((steps, 2)),
            dma((2, 8)), dma((2, 8)),
            dma((steps, 2)), dma((steps, 2)),
            dma((steps, 3)), dma((steps, 3)),
            dma((steps, 7)), dma((steps, 7)),
            dma((steps, 7)), dma((steps, 7)),
        ],
        compiler_params=pltpu.CompilerParams(
            collective_id=0, has_side_effects=True, vmem_limit_bytes=56 * 1024 * 1024
        ),
    )(tile_rows[0], tile_cols[0], tile_count, entries, block_x, block_y)


def solution(mesh):
    placed = (
        P("row", "col", None, None, None),
        P("row", "col", None),
        P("row", "col", None),
        P("row", "col"),
        P(None, ("row", "col")),
        P(None, ("row", "col")),
    )
    return jax.shard_map(
        local, mesh=mesh, in_specs=placed, out_specs=(P(), P(None, ("row", "col"))), check_vma=False
    )
```

```python
import functools

import jax
import jax.numpy as jnp
from jax import lax
from jax.experimental import pallas as pl
from jax.experimental.pallas import tpu as pltpu
from jax.sharding import PartitionSpec as P

STEP_COUNT = 3
MODULUS = 65521.0
INVERSE = 1.0 / 65521.0
MESH = pl.DeviceIdType.MESH
NX, NYL, NYH, NZ = 4, 4, 2, 8
DIRECT = (0, 1, 2, 3)
F32, I32, BF16 = jnp.float32, jnp.int32, jnp.bfloat16


def reduce_mod(values):
    leftover = values - jnp.floor(values * INVERSE) * MODULUS
    leftover = jnp.where(leftover < 0, leftover + MODULUS, leftover)
    return jnp.where(leftover >= MODULUS, leftover - MODULUS, leftover)


def split_digits(values):
    high_digit = jnp.floor(values * (1.0 / 256.0))
    return (high_digit, values - 256.0 * high_digit)


def fold(values):
    high = values >> 16
    return (high << 4) - high + (values & 65535)


def times15(values):
    return (values << 4) - values


def kernel(
    rows_ref, cols_ref, count_ref, entries_ref, x_ref, y_ref, c_ref, v_ref,
    ent, adig, xdig, gat, vdig, prods, part, lbuf, sbuf, ybuf, ysrc, vbuf, xall, cloc, chalf, crecv, axb, ayb, azb, cfull, xall_digits, tables, table,
    table_sem, ent_sem, ys, yr, xs, xr, rs, rr, bs, br, ls, lr, hs, hr, ps, pr, qs, qr, cs, cr, axs, axr, ays, ayr, azs, azr,
):
    row, col = lax.axis_index("row"), lax.axis_index("col")
    core, yl, px = row % 2, (row // 2) % NYL, row // (2 * NYL)
    yh, pz = col // NZ, col % NZ
    step_r = 1 - 2 * core

    def rid(ax, ay, ac):
        return (((ax + 2 * NX) % NX) * NYL + (ay + 2 * NYL) % NYL) * 2 + ac

    def dev_x(d):
        return (rid(px + d, yl, core), col)

    def dev_y(d):
        whole = (yh * NYL + yl + d) % (NYL * NYH)
        return (rid(px, whole % NYL, core), (whole // NYL) * NZ + pz)

    def dev_z(d):
        return (row, yh * NZ + (pz + d + 2 * NZ) % NZ)

    sibling = (rid(px, yl, 1 - core), col)

    def remote(src, dst, ssem, rsem, dev):
        return pltpu.make_async_remote_copy(
            src_ref=src, dst_ref=dst, send_sem=ssem, recv_sem=rsem, device_id=dev, device_id_type=MESH
        )

    tile_total = ent.shape[0]
    chunk = 8

    def entry_copy(n):
        where = pl.ds(n * chunk, chunk)
        return pltpu.make_async_copy(entries_ref.at[where], ent.at[where], ent_sem.at[n])

    for n in range(tile_total // chunk):
        entry_copy(n).start()

    barrier = pltpu.get_barrier_semaphore()
    partners = [dev_x(d) for d in range(1, NX)] + [dev_y(d) for d in range(1, 8)]
    partners += [dev_z(d) for d in range(1, NZ)] + [sibling]
    for partner in partners:
        pl.semaphore_signal(barrier, inc=1, device_id=partner, device_id_type=MESH)

    high_x, low_x = split_digits(x_ref[...])
    xdig[0:64, :] = high_x.astype(BF16)
    xdig[64:128, :] = low_x.astype(BF16)
    vbuf[0] = y_ref[...]
    pl.semaphore_wait(barrier, len(partners))

    def gather(i, between):
        own = vbuf.at[i]
        sends = []

        def send(src, dst, ssem, rsem, dev):
            copy = remote(src, dst, ssem, rsem, dev)
            copy.start()
            sends.append(copy)

        def piece(r):
            return gat.at[i, r]

        def arrive(r, rsem):
            remote(piece(r), piece(r), bs.at[i, 0], rsem, sibling).wait_recv()

        def both_x(src, r, d):
            send(src, piece(r), xs.at[i, d, 0], xr.at[i, d, 0], dev_x(1))
            send(src, piece(r), xs.at[i, d, 1], xr.at[i, d, 1], dev_x(-1))
            if d in DIRECT:
                send(src, piece(r), rs.at[i, d], rr.at[i, d], dev_x(2))

        def to_sibling(src, r, n):
            send(src, piece(r), bs.at[i, n], br.at[i, n], sibling)

        for d in range(1, NYL):
            target = (rid(px, yl + d, core), col)
            send(own, piece(row), ys.at[i, d - 1], yr.at[i, d - 1], target)
        both_x(own, row, 0)
        to_sibling(own, row, 0)
        gat[i, row] = vbuf[i]
        between(0)

        def relay(d):
            near = rid(px - step_r, yl - d, core)
            arrive(near, xr.at[i, d, core])
            if d not in DIRECT:
                send(piece(near), piece(near), rs.at[i, d], rr.at[i, d], dev_x(step_r))
            to_sibling(piece(near), near, 4 + d)

        for d in range(1, NYL):
            r = rid(px, yl - d, core)
            arrive(r, yr.at[i, d - 1])
            both_x(piece(r), r, d)
            to_sibling(piece(r), r, d)
            relay(d - 1)
            between(d)
        relay(NYL - 1)
        for d in range(NYL):
            other = rid(px + step_r, yl - d, core)
            arrive(other, xr.at[i, d, 1 - core])
            to_sibling(piece(other), other, 8 + d)
            far = rid(px + 2, yl - d, core)
            arrive(far, rr.at[i, d])
            to_sibling(piece(far), far, 12 + d)
        for n in range(16):
            shift = (0, step_r, -step_r, 2)[n // 4]
            arrive(rid(px + shift, yl - n % 4, 1 - core), br.at[i, n])
        for copy in sends:
            copy.wait_send()

    def make_tables():
        shape = (tile_total, tile_total)
        down, across = lax.broadcasted_iota(I32, shape, 0), lax.broadcasted_iota(I32, shape, 1)

        def upright(flat):
            return jnp.sum(jnp.where(down == across, flat, 0), 1, keepdims=True)

        def add_up(values):
            return jnp.sum(values, 0, keepdims=True)

        tables[...] = jnp.zeros((8, 128), I32)
        live = across < count_ref[0, 0]
        flat_keys = jnp.where(live, jnp.broadcast_to(rows_ref[...], shape), 32)
        keys = upright(flat_keys)
        earlier = (flat_keys == keys) & (across < down)
        rank = jnp.sum(((flat_keys < keys) | earlier).astype(I32), 1, keepdims=True)
        repeated = jnp.max(earlier.astype(I32), 1, keepdims=True)
        chosen = rank == across
        columns = upright(jnp.broadcast_to(cols_ref[...], shape))
        tables[0:1, 0:64] = add_up(jnp.where(chosen, down, 0))
        tables[1:2, 0:64] = add_up(jnp.where(chosen, columns, 0))
        tables[2:3, 0:64] = add_up(jnp.where(chosen, -repeated, 0))
        tables[3:4, 0:64] = jnp.maximum(add_up((keys <= across).astype(I32)) - 1, 0)
        tables[4:5, 0:64] = -jnp.max((keys == across).astype(I32), 0, keepdims=True)
        return pltpu.make_async_copy(tables, table, table_sem)

    def make_digits(n):
        @pl.loop(n * chunk, (n + 1) * chunk)
        def _(t):
            high, low = split_digits(ent[t].T)
            adig[t, :, 0:128] = high.astype(BF16)
            adig[t, :, 128:256] = low.astype(BF16)

    def nothing(stage):
        del stage

    def first_between(stage):
        if stage == 0:
            moved = make_tables()
            moved.start()
            moved.wait()
        for n in (2 * stage, 2 * stage + 1):
            entry_copy(n).wait()
            make_digits(n)

    def multiply(i):
        @pl.loop(0, 32)
        def _(r):
            high, low = split_digits(gat[i, r])
            for j in range(2):
                vdig[2 * r + j, 0:64, :] = high[:, j * 128 : (j + 1) * 128].astype(BF16)
                vdig[2 * r + j, 64:128, :] = low[:, j * 128 : (j + 1) * 128].astype(BF16)

        width = 32

        def body(n, total):
            for u in range(width):
                j = n * width + u
                p = jnp.dot(vdig[table[1, j]], adig[table[0, j]], preferred_element_type=F32)
                middle = p[0:64, 128:256] + p[64:128, 0:128]
                product = jnp.concatenate([middle, p[0:64, 0:128], p[64:128, 128:256]], 0)
                total = (total & table[2, j]) + product.astype(I32)
                prods[j] = total
            return total

        lax.fori_loop(0, tile_total // width, body, jnp.zeros((192, 128), I32))

    def slot_of(z, q):
        return (yh if q else 1 - yh) * NZ + (z + 2 * NZ) % NZ

    def fill(slot):
        for j in range(2):
            b = 2 * slot + j
            sums = prods[table[3, b]] & table[4, b]
            total = times15(fold(sums[64:128])) + (fold(sums[0:64]) << 8) + sums[128:192]
            rest = fold(total).astype(F32)
            part[slot, :, j * 128 : (j + 1) * 128] = rest - jnp.floor(rest * INVERSE) * MODULUS

    def reduce(i, between):
        sends = []

        def long_copy(src, k, q):
            return remote(src, lbuf.at[i, k, q], ls.at[i, k, q], lr.at[i, k, q], dev_z(step_r))

        def short_copy(src, k, q):
            return remote(src, sbuf.at[i, k, q], hs.at[i, k, q], hr.at[i, k, q], dev_z(-step_r))

        def start(copy):
            copy.start()
            sends.append(copy)

        def own(z, q):
            return part.at[slot_of(z, q // 2), pl.ds(32 * (q % 2), 32)]

        for q in range(4):
            if q % 2 == 0:
                fill(slot_of(pz + 4, q // 2))
            start(long_copy(own(pz + 4, q), 0, q))
            if q % 2 == 0:
                fill(slot_of(pz - 3 * step_r, q // 2))
            start(short_copy(own(pz - 3 * step_r, q), 0, q))
        for shift in (3, -2, 2, -1, 1, 0):
            for q in range(2):
                fill(slot_of(pz + shift * step_r, q))
        between(0)
        for k in range(3):
            for q in range(4):
                mine_here = own(pz + (3 - k) * step_r, q)
                long_copy(mine_here, k, q).wait_recv()
                lbuf[i, k, q] = lbuf[i, k, q] + mine_here[...]
                start(long_copy(lbuf.at[i, k, q], k + 1, q))
                if k < 2:
                    mine_here = own(pz - (2 - k) * step_r, q)
                    short_copy(mine_here, k, q).wait_recv()
                    sbuf[i, k, q] = sbuf[i, k, q] + mine_here[...]
                    start(short_copy(sbuf.at[i, k, q], k + 1, q))
            between(k + 1)
        swaps = []
        wholes = []
        for q in range(4):
            mine_here = own(pz, q)
            short_copy(mine_here, 2, q).wait_recv()
            long_copy(mine_here, 3, q).wait_recv()
            whole = lbuf[i, 3, q] + sbuf[i, 2, q] + mine_here[...]
            if q < 2:
                ysrc[i, q] = whole
                swaps.append(remote(ysrc.at[i, q], ybuf.at[i, q], ps.at[i, q], pr.at[i, q], dev_y(4)))
                swaps[-1].start()
            else:
                wholes.append(whole)
        between(4)
        for q in range(2):
            swaps[q].wait_recv()
            vbuf[i + 1, pl.ds(32 * q, 32)] = reduce_mod(wholes[q] + ybuf[i, q])
        sends.extend(swaps)
        return sends

    left_half = lax.broadcasted_iota(I32, (64, 128), 1) < 64

    def quads(products):
        upper, lower = products[0:64], pltpu.roll(products[64:128], 64, 1)
        mixed = jnp.where(left_half, times15(fold(upper)) + lower, fold(upper + lower) << 8)
        return reduce_mod(fold(mixed + pltpu.roll(mixed, 64, 1)).astype(F32))

    def stacked(values):
        high, low = split_digits(values)
        return jnp.concatenate([high.astype(BF16), low.astype(BF16)], 0)

    def project(x_digits, values):
        return lax.dot_general(
            x_digits, stacked(values), (((1,), (1,)), ((), ())), preferred_element_type=F32
        ).astype(I32)

    def keep_terms(i, products):
        residues = quads(products)
        cloc[i] = jnp.where(left_half[0:32], residues[0:32], residues[32:64])

    mine = pl.ds(16 * core, 16)
    theirs = pl.ds(16 - 16 * core, 16)
    pending = []

    def sum_stages(i):
        first = remote(cloc.at[i, theirs], crecv.at[i], cs.at[i, 0], cr.at[i, 0], sibling)
        last = remote(chalf.at[i, 3], cfull.at[i, mine], cs.at[i, 1], cr.at[i, 1], sibling)

        def copies(k, count, landing, ssem, rsem, dev):
            return [
                remote(chalf.at[i, k], landing.at[i, d - 1], ssem.at[i, d - 1], rsem.at[i, d - 1], dev(d))
                for d in range(1, count)
            ]

        rounds = [
            (copies(0, NX, axb, axs, axr, dev_x), axb),
            (copies(1, NYL * NYH, ayb, ays, ayr, dev_y), ayb),
            (copies(2, NZ, azb, azs, azr, dev_z), azb),
        ]

        def begin(k):
            for copy in rounds[k][0]:
                copy.start()
            pending.extend(rounds[k][0])

        def finish(k):
            total = chalf[i, k]
            for d, copy in enumerate(rounds[k][0]):
                copy.wait_recv()
                total = total + rounds[k][1][i, d]
            chalf[i, k + 1] = total if k == 0 else reduce_mod(total)

        def stage(n):
            if n == 0:
                first.start()
                pending.append(first)
            elif n == 1:
                first.wait_recv()
                chalf[i, 0] = cloc[i, mine] + crecv[i]
                begin(0)
            elif n < 4:
                finish(n - 2)
                begin(n - 1)
            elif n == 4:
                finish(2)
                last.start()
                pending.append(last)
                cfull[i, mine] = chalf[i, 3]
            else:
                last.wait_recv()

        return stage

    def twice(i):
        packed = cfull[i]
        turned = pltpu.roll(packed, 64, 1)
        return jnp.concatenate(
            [jnp.where(left_half[0:32], packed, turned), jnp.where(left_half[0:32], turned, packed)], 0
        )

    def times(left, right):
        left_digits = stacked(left)[:, 0:64]
        high, low = split_digits(right)
        right_digits = jnp.where(left_half, high, low).astype(BF16)
        return quads(jnp.dot(left_digits, right_digits, preferred_element_type=F32).astype(I32))

    def send_x(source, where, k):
        copies = []
        for d in range(1, NZ):
            copies.append(remote(source, xall.at[where], qs.at[k, d], qr.at[k, d], dev_z(d)))
            copies[-1].start()
        pending.extend(copies)

    partner_col = (1 - yh) * NZ + pz
    x_swap = remote(x_ref, xall.at[col], qs.at[0, 0], qr.at[0, 0], dev_y(4))
    x_swap.start()
    pending.append(x_swap)
    send_x(x_ref, col, 0)
    xall[col] = x_ref[...]

    stages = [sum_stages(i) for i in range(STEP_COUNT)]

    gather(0, first_between)
    multiply(0)
    sends = reduce(0, nothing)
    remote(x_ref, xall.at[partner_col], qs.at[0, 0], qr.at[0, 0], dev_y(4)).wait_recv()

    def second_between(stage):
        if stage == 0:
            send_x(xall.at[partner_col], partner_col, 1)
            keep_terms(0, project(xdig[...], vbuf[1]))
        stages[0](stage)

    def second_reduce(stage):
        if stage == 0:
            stages[0](4)
        if stage == 1:
            stages[0](5)

    gather(1, second_between)
    multiply(1)
    for copy in sends:
        copy.wait_send()
    sends = reduce(1, second_reduce)

    def receive_x():
        for k in range(2):
            for d in range(1, NZ):
                where = (yh if k == 0 else 1 - yh) * NZ + (pz - d + NZ) % NZ
                remote(x_ref, xall.at[where], qs.at[k, d], qr.at[k, d], dev_z(d)).wait_recv()

    def third_between(stage):
        if stage == 0:
            keep_terms(1, project(xdig[...], vbuf[2]))
            receive_x()
        for slot in range(4 * stage, 4 * stage + 4):
            xall_digits[slot] = stacked(xall[slot])
        stages[1](stage)

    gather(2, third_between)
    stages[1](4)
    multiply(2)
    stages[1](5)
    for copy in sends:
        copy.wait_send()
    known = {}

    def third_reduce(stage):
        if stage == 0:
            total = jnp.zeros((128, 128), I32)
            for slot in range(16):
                total = total + project(xall_digits[slot], part[slot])
            keep_terms(2, total)
            stages[2](0)
            first, second = twice(0), twice(1)
            known["zero"] = reduce_mod(-first)
            error = reduce_mod(times(known["zero"], second) + first)
            known["one"] = reduce_mod(known["zero"] - error)
            known["zero"] = reduce_mod(-times(error, known["zero"]))
            known["rest"] = times(known["one"], second) + first
            stages[2](1)
        else:
            stages[2](stage + 1)

    sends = reduce(2, third_reduce)
    v_ref[...] = vbuf[STEP_COUNT] / MODULUS
    error = reduce_mod(times(known["zero"], twice(2)) + known["rest"])
    c_ref[0] = (reduce_mod(-times(error, known["zero"])) / MODULUS)[:, 0:64]
    c_ref[1] = (reduce_mod(known["zero"] - times(error, known["one"])) / MODULUS)[:, 0:64]
    c_ref[2] = (reduce_mod(known["one"] - error) / MODULUS)[:, 0:64]
    for copy in sends + pending:
        copy.wait_send()


def local(tile_entries, tile_rows, tile_cols, tile_count, block_x, block_y):
    entries = tile_entries[0, 0]
    slots = entries.shape[0]
    vmem = pl.BlockSpec(memory_space=pltpu.VMEM)
    smem = pl.BlockSpec(memory_space=pltpu.SMEM)
    steps = STEP_COUNT
    dma = pltpu.SemaphoreType.DMA
    return pl.pallas_call(
        kernel,
        out_shape=(
            jax.ShapeDtypeStruct((steps, 64, 64), F32),
            jax.ShapeDtypeStruct((64, 256), F32),
        ),
        in_specs=[vmem, vmem, smem, pl.BlockSpec(memory_space=pl.ANY), vmem, vmem],
        out_specs=(vmem, vmem),
        scratch_shapes=[
            pltpu.VMEM((slots, 128, 128), F32),
            pltpu.VMEM((slots, 128, 256), BF16),
            pltpu.VMEM((128, 256), BF16),
            pltpu.VMEM((steps, 32, 64, 256), F32),
            pltpu.VMEM((64, 128, 128), BF16),
            pltpu.VMEM((slots, 192, 128), I32),
            pltpu.VMEM((16, 64, 256), F32),
            pltpu.VMEM((steps, 4, 4, 32, 256), F32),
            pltpu.VMEM((steps, 3, 4, 32, 256), F32),
            pltpu.VMEM((steps, 2, 32, 256), F32),
            pltpu.VMEM((steps, 2, 32, 256), F32),
            pltpu.VMEM((steps + 1, 64, 256), F32),
            pltpu.VMEM((16, 64, 256), F32),
            pltpu.VMEM((steps, 32, 128), F32),
            pltpu.VMEM((steps, 4, 16, 128), F32),
            pltpu.VMEM((steps, 16, 128), F32),
            pltpu.VMEM((steps, NX - 1, 16, 128), F32),
            pltpu.VMEM((steps, 7, 16, 128), F32),
            pltpu.VMEM((steps, 7, 16, 128), F32),
            pltpu.VMEM((steps, 32, 128), F32),
            pltpu.VMEM((16, 128, 256), BF16),
            pltpu.VMEM((8, 128), I32),
            pltpu.SMEM((8, 128), I32),
            dma(()),
            dma((8,)),
            dma((steps, 3)), dma((steps, 3)),
            dma((steps, 4, 2)), dma((steps, 4, 2)),
            dma((steps, 4)), dma((steps, 4)),
            dma((steps, 16)), dma((steps, 16)),
            dma((steps, 4, 4)), dma((steps, 4, 4)),
            dma((steps, 3, 4)), dma((steps, 3, 4)),
            dma((steps, 2)), dma((steps, 2)),
            dma((2, 8)), dma((2, 8)),
            dma((steps, 2)), dma((steps, 2)),
            dma((steps, 3)), dma((steps, 3)),
            dma((steps, 7)), dma((steps, 7)),
            dma((steps, 7)), dma((steps, 7)),
        ],
        compiler_params=pltpu.CompilerParams(
            collective_id=0, has_side_effects=True, vmem_limit_bytes=56 * 1024 * 1024
        ),
    )(tile_rows[0], tile_cols[0], tile_count, entries, block_x, block_y)


def solution(mesh):
    placed = (
        P("row", "col", None, None, None),
        P("row", "col", None),
        P("row", "col", None),
        P("row", "col"),
        P(None, ("row", "col")),
        P(None, ("row", "col")),
    )
    return jax.shard_map(
        local, mesh=mesh, in_specs=placed, out_specs=(P(), P(None, ("row", "col"))), check_vma=False
    )
```
